256 devices in a mesh: band: 64 (over z, y, core), tile: 4 (over x).
Axes of the slice: x: 4, y: 4, z: 8, core: 2. Of those that a mesh axis runs over, the one named last changes fastest.
Arguments:
- src_field: bfloat16 [4, 32, 1048576], P(None, None, ('band', 'tile')), may hold values from 0.0009994507 to 1
- weights: bfloat16 [65536, 128, 128], P(('band', 'tile')), may hold values from 0 to 0.05625
- block_slab: int32 [65536], P(('band', 'tile')), may hold values from 0 to 127
- block_dest: int32 [65536, 1], P(('band', 'tile')), may hold values from 0 to 255; in each aligned block of 256 rows (0 to 255, 256 to 511, ...) at most 2 rows name the same one
- block_tile: int32 [65536], P(('band', 'tile')), may hold values from 0 to 31
- prior_total: float32 [32, 1048576], P(None, ('band', 'tile')), may hold values from 0.2 to 4
- gamma_shape: float32 [1048576], P(('band', 'tile')), may hold values from 1 to 10
- gamma_scale: float32 [1048576], P(('band', 'tile')), may hold values from 0.05 to 0.6
Outputs:
- season_total: float32 [32, 1048576], P(None, ('band', 'tile'))
- spi_index: float32 [32, 1048576], P(None, ('band', 'tile'))
The draws below stay inside these ranges and needn't reach their ends.
Inputs may be any that keep to these rules, and one draw needn't show every extreme that they name: `block_dest`: among the 256 blocks of any one device, each destination is named by at most 2 blocks, a bound that some block reaches.
All inputs are finite; a program needn't handle non-finite values.
Results may differ from the reference program's by a relative error of at most 0.00085.
Values may be sent and summed in bfloat16 or wider, within the bound.
A program may use at most 128 MiB of HBM per device.

```python
import math
import jax
import jax.numpy as jnp
import numpy as np
from jax import lax

DAYS = 4
MEM = 32
TILE_DEV = 32
INTERSECTION = 8
SLAB_DEV = 32
BLK_DEV = 256
CAP = 2
SRC = 1048576
TGT = 1048576
BLOCKS = 65536
N_BAND = 64
N_TILE = 4


def draw_weights(key, part):
    key_offset = jax.random.fold_in(key, 11)
    key_span = jax.random.fold_in(key, 23)
    key_factor = jax.random.fold_in(key, 37)
    offset = jax.random.randint(key_offset, (BLOCKS, 1, 128), 0, 128)
    span = jax.random.randint(key_span, (BLOCKS, 1, 128), 4, 9)
    source_rows = jnp.arange(128, dtype=jnp.int32)[None, :, None]
    inside = jnp.mod(source_rows - offset, 128) < span
    factor = jax.random.uniform(key_factor, (BLOCKS, 128, 128), jnp.float32, 0.2, 1.8)
    values = jnp.where(inside, factor / (INTERSECTION * span.astype(jnp.float32)), jnp.float32(0.0))
    return values.astype(jnp.bfloat16)


def set_ends(values, own_key, least, top_value):
    extent = values.shape
    spot = [jax.random.randint(jax.random.fold_in(own_key, axis), (), 0, extent[axis]) for axis in range(len(extent))]
    values = values.at[tuple(spot)].set(least)
    longest = extent.index(max(extent))
    spot[longest] = (spot[longest] + 1) % extent[longest]
    return values.at[tuple(spot)].set(top_value)


def steps_of(key, shape, split, smallest, high):
    def one(axis_at, blocks):
        draws = jax.random.uniform(jax.random.fold_in(jax.random.fold_in(key, 6), axis_at), (blocks,), jnp.float32, smallest / len(split), high / len(split))
        return jnp.repeat(jnp.exp(draws), shape[axis_at] // blocks).reshape((-1,) + (1,) * (len(shape) - axis_at - 1))

    gain = one(*split[0])
    for cut in split[1:]:
        gain = gain * one(*cut)
    return gain


def shared_out(stream_key, own, number, rows, count, top, most, skew):
    ranking = jax.random.permutation(stream_key, count)
    packed, usual = load_shares(count, rows * top, most, skew, True), load_shares(count, rows * top, most, skew, False)
    places = jnp.arange(count)

    def named(lengths, offset_by):
        used = int((lengths > 0).sum())
        fixed = max(1, used // 4)
        shifted = fixed + (places - fixed + offset_by * (used - fixed)) % max(1, count - fixed)
        return jnp.zeros((count,), jnp.int32).at[ranking[jnp.where(places < fixed, places, shifted)]].set(jnp.asarray(lengths, jnp.int32))

    lengths = jnp.where(number % 4 == 0, named(packed, number // 4), named(usual, number - number // 4 - 1))
    mixed = jax.random.permutation(jax.random.fold_in(own, 3), count)
    source_of, sink = mixed[0:count // 2 * 2:2], mixed[1:count // 2 * 2:2]
    room = jnp.minimum(lengths[source_of] - 1, most - lengths[sink]) // 2
    room = jnp.where((source_of == ranking[0]) | (sink == ranking[0]) | (lengths[sink] == 0), 0, jnp.maximum(room, 0))
    shifted = jax.random.randint(jax.random.fold_in(own, 4), (count // 2,), 0, 1 << 20) % (room + 1)
    lengths = lengths.at[source_of].add(-shifted).at[sink].add(shifted)
    members = jnp.searchsorted(jnp.cumsum(lengths), jnp.arange(rows * top), side="right").astype(jnp.int32)
    grid = members.reshape(top, rows).T
    grid = grid[jax.random.permutation(jax.random.fold_in(own, 1), rows)]
    offset_by = jax.random.randint(jax.random.fold_in(own, 2), (rows, 1), 0, top)
    return jnp.take_along_axis(grid, (jnp.arange(top)[None, :] + offset_by) % top, axis=1)


def load_shares(count, total, most, slope, full):
    weights = [(1 << 20) // math.isqrt(standing ** slope) + 1 for standing in range(1, count + 1)]
    largest = most if full else min(most, max(-(-total // count), total * weights[0] // sum(weights)))
    least = 1 if total - largest >= count - 1 else 0
    given, spare = [largest] + [least] * (count - 1), total - largest - least * (count - 1)
    while spare > 0:
        free = [i for i in range(1, count) if given[i] < largest] or [i for i in range(1, count) if given[i] < most]
        pool, remaining = sum([weights[i] for i in free]), spare
        for i in free:
            more = min(most - given[i], max(1, remaining * weights[i] // pool), spare)
            given[i] = given[i] + more
            spare = spare - more
    return np.array(given)


def setup_inputs(seed: int = 0) -> dict:
    seeds = jax.random.split(jax.random.key(seed), 9)
    src_field = jnp.clip(jnp.exp(math.log(1.0) - 6.9083047 * jax.random.uniform(seeds[0], (DAYS, MEM, SRC), jnp.float32) ** steps_of(seeds[0], (DAYS, MEM, SRC), ((2, 256),), -0.2, 0.2)), 0.0009994507, 1.0).astype(jnp.bfloat16)
    weights = draw_weights(jax.random.fold_in(seeds[8], 71), 0)
    block_slab = set_ends(jax.random.randint(seeds[2], (BLOCKS,), 0, N_TILE * SLAB_DEV), jax.random.fold_in(seeds[2], 1), 0, (N_TILE * SLAB_DEV) - 1).astype(jnp.int32)
    block_dest_keys = jax.random.split(jax.random.fold_in(seeds[3], 1), BLOCKS // BLK_DEV)
    block_dest_turns = jax.random.permutation(jax.random.fold_in(seeds[3], 3), BLOCKS // BLK_DEV)
    block_dest = jax.vmap(lambda own, number: shared_out(jax.random.fold_in(seeds[3], 2), own, number, BLK_DEV, N_BAND * N_TILE, 1, CAP, 2))(block_dest_keys, block_dest_turns).reshape((BLOCKS, 1))
    block_tile = set_ends(jax.random.randint(seeds[4], (BLOCKS,), 0, TILE_DEV), jax.random.fold_in(seeds[4], 1), 0, TILE_DEV - 1).astype(jnp.int32)
    prior_total = jnp.clip(0.2 + 3.8 * jax.random.uniform(seeds[5], (MEM, TGT), jnp.float32) ** steps_of(seeds[5], (MEM, TGT), ((1, 256),), -0.2, 0.2), 0.2, 4.0)
    gamma_shape = jnp.clip(jnp.exp(math.log(10.0) - 2.3025851 * jax.random.uniform(seeds[6], (TGT,), jnp.float32) ** steps_of(seeds[6], (TGT,), ((0, 256),), -0.2, 0.2)), 1.0, 10.0)
    gamma_scale = jnp.clip(jnp.exp(math.log(0.6) - 2.4849067 * jax.random.uniform(seeds[7], (TGT,), jnp.float32) ** steps_of(seeds[7], (TGT,), ((0, 256),), -0.2, 0.2)), 0.05, 0.6)
    return {"src_field": src_field, "weights": weights, "block_slab": block_slab, "block_dest": block_dest, "block_tile": block_tile, "prior_total": prior_total, "gamma_shape": gamma_shape, "gamma_scale": gamma_scale}


PROB_FLOOR = 0.001
CENTRAL_NUMER = (-39.69683028665376, 220.9460984245205, -275.9285104469687, 138.357751867269, -30.66479806614716, 2.506628277459239)
CENTRAL_DENOM = (-54.47609879822406, 161.5858368580409, -155.6989798598866, 66.80131188771972, -13.28068155288572, 1.0)
TAIL_NUMER = (-0.007784894002430293, -0.3223964580411365, -2.400758277161838, -2.549671010429402, 4.374664141464968, 2.938163982698783)
TAIL_DENOM = (0.007784695709041462, 0.3224671290700398, 2.445134137142996, 3.754408661907416, 1.0)

def horner(coeffs, value):
    total = jnp.zeros_like(value) + coeffs[0]
    for coeff in coeffs[1:]:
        total = total * value + coeff
    return total

def normal_quantile(prob):
    centred = prob - 0.5
    square = centred * centred
    middle = centred * horner(CENTRAL_NUMER, square) / horner(CENTRAL_DENOM, square)
    lower_root = jnp.sqrt(-2.0 * jnp.log(prob))
    lower = horner(TAIL_NUMER, lower_root) / horner(TAIL_DENOM, lower_root)
    upper_root = jnp.sqrt(-2.0 * jnp.log(1.0 - prob))
    upper = -horner(TAIL_NUMER, upper_root) / horner(TAIL_DENOM, upper_root)
    result = jnp.where(prob < 0.02425, lower, middle)
    return jnp.where(prob > 0.97575, upper, result)

def lower_gamma(shape, value):
    border = shape + 1.0
    small_x = jnp.minimum(value, border)
    large_x = jnp.maximum(value, border)

    def series_step(index, carry):
        term, total = carry
        term = term * small_x / (shape + index)
        return (term, total + term)
    first = 1.0 / shape
    _, series = lax.fori_loop(1, 65, series_step, (first, first))
    series_value = series * jnp.exp(-small_x + shape * jnp.log(small_x) - lax.lgamma(shape))
    start_b = large_x + 1.0 - shape
    start_c = jnp.zeros_like(large_x) + 1e+30
    start_d = 1.0 / start_b

    def fraction_step(index, carry):
        denom_b, lentz_c, lentz_d, accum = carry
        step_a = -index * (index - shape)
        denom_b = denom_b + 2.0
        lentz_d = 1.0 / (step_a * lentz_d + denom_b)
        lentz_c = denom_b + step_a / lentz_c
        return (denom_b, lentz_c, lentz_d, accum * lentz_d * lentz_c)
    _, _, _, fraction = lax.fori_loop(1, 65, fraction_step, (start_b, start_c, start_d, start_d))
    upper_value = fraction * jnp.exp(-large_x + shape * jnp.log(large_x) - lax.lgamma(shape))
    return jnp.where(value < border, series_value, 1.0 - upper_value)

def reference(src_field, weights, block_slab, block_dest, block_tile, prior_total, gamma_shape, gamma_scale):
    devices = N_BAND * N_TILE
    grouped = src_field.reshape(DAYS, MEM, N_BAND, N_TILE * SLAB_DEV, 128)
    block_weights = weights.reshape(devices, BLK_DEV, 128, 128)
    slab_ids = block_slab.reshape(devices, BLK_DEV)
    owner_ids = block_dest.reshape(devices, BLK_DEV)
    tile_ids = block_tile.reshape(devices, BLK_DEV)

    def add_device(totals, device):
        band_id = (device // N_TILE).astype(jnp.int32)
        owned = lax.dynamic_index_in_dim(grouped, band_id, axis=2, keepdims=False)
        chosen = jnp.take(owned, slab_ids[device], axis=2).astype(jnp.float32)
        pieces = jnp.einsum('dmbs,bst->bmt', chosen, block_weights[device].astype(jnp.float32), precision=lax.Precision.HIGHEST)
        target = owner_ids[device] * TILE_DEV + tile_ids[device]
        return (totals.at[target].add(pieces), None)
    start = jnp.zeros((devices * TILE_DEV, MEM, 128), jnp.float32)
    totals, _ = lax.scan(add_device, start, jnp.arange(devices, dtype=jnp.int32))
    remapped = jnp.transpose(totals, (1, 0, 2)).reshape(MEM, devices * TILE_DEV * 128)
    season_total = prior_total + remapped
    shape_full = jnp.broadcast_to(gamma_shape[None, :], season_total.shape)
    probability = lower_gamma(shape_full, season_total / gamma_scale[None, :])
    probability = jnp.clip(probability, PROB_FLOOR, 1.0 - PROB_FLOOR)
    spi_index = normal_quantile(probability)
    return (season_total, spi_index)
```

```python
import functools

import jax
import jax.numpy as jnp
from jax import lax
from jax.experimental import pallas as pl
from jax.experimental.pallas import tpu as pltpu
from jax.sharding import PartitionSpec as P

MESH = pl.DeviceIdType.MESH
F32, BF16, I32 = jnp.float32, jnp.bfloat16, jnp.int32

PROB_FLOOR = 0.001
CENTRAL_NUMER = (
    -39.69683028665376,
    220.9460984245205,
    -275.9285104469687,
    138.357751867269,
    -30.66479806614716,
    2.506628277459239,
)
CENTRAL_DENOM = (
    -54.47609879822406,
    161.5858368580409,
    -155.6989798598866,
    66.80131188771972,
    -13.28068155288572,
    1.0,
)
TAIL_NUMER = (
    -0.007784894002430293,
    -0.3223964580411365,
    -2.400758277161838,
    -2.549671010429402,
    4.374664141464968,
    2.938163982698783,
)
TAIL_DENOM = (0.007784695709041462, 0.3224671290700398, 2.445134137142996, 3.754408661907416, 1.0)

NZ, NY, NC, NX = 8, 4, 2, 4
PLANE = NY * NC * NX
DAYS, MEM, TILES, SLABS, BLOCKS = 4, 32, 32, 32, 256
SLOTS = 2 * NZ
ALL_SLABS = NX * SLABS
CHUNKS = 8
MC = MEM // CHUNKS
HALF = NZ // 2
FRACTION_TOP = 512.0
EMPTY = ALL_SLABS << 5
LANCZOS_BASE = 0.99999999999980993227684700473478
LANCZOS = (
    676.520368121885098567009190444019,
    -1259.13921672240287047156078755283,
    771.3234287776530788486528258894,
    -176.61502916214059906584551354,
    12.507343278686904814458936853,
    -0.13857109526572011689554707,
    9.984369578019570859563e-6,
    1.50563273514931155834e-7,
)


def horner(coeffs, value):
    total = coeffs[0]
    for coeff in coeffs[1:]:
        total = total * value + coeff
    return total


def log_gamma(shape):
    less = shape - 1.0
    total = LANCZOS_BASE
    for i, coeff in enumerate(LANCZOS):
        total = total + coeff / (less + float(i + 1))
    shifted = less + 7.5
    return 0.9189385332046727 + (less + 0.5) * jnp.log(shifted) - shifted + jnp.log(total)


def drain(ref, sem):
    pltpu.make_async_copy(ref, ref, sem).wait()


def kernel(
    slab_ref, dest_ref, tile_ref, src_hbm, w_hbm, prior_hbm, shape_ref, scale_ref,
    season_hbm, spi_hbm,
    src_ref, prior_ref, season_ref, spi_ref, table_vmem, table, label_ref, lgamma_ref,
    slabs, w_vmem, stage, sendb, recvb, labels, onehot, part, rs_send, rs_recv, series, prior_rows, season_rows, spi_rows,
    w_sem, src_sem, prior_sem, table_sem, out_sem, ag_send, ag_recv, lab_send, lab_recv, p1_send, p1_recv, rs_send_sem, rs_recv_sem,
):
    band = lax.axis_index("band")
    x = lax.axis_index("tile")
    core = band % NC
    y = (band // NC) % NY
    z = band // (NC * NY)
    me = (y * NC + core) * NX + x

    def peer(offset):
        y2 = (y + offset // (NC * NX)) % NY
        c2 = (core + (offset // NX) % NC) % NC
        x2 = (x + offset % NX) % NX
        return (y2 * NC + c2) * NX + x2, ((z * NY + y2) * NC + c2, x2)

    def z_device(z2):
        return ((z2 * NY + y) * NC + core, x)

    up, down = z_device((z + 1) % NZ), z_device((z + NZ - 1) % NZ)

    src_copy = pltpu.make_async_copy(src_hbm, src_ref, src_sem)
    src_copy.start()
    barrier = pltpu.get_barrier_semaphore()

    def greet(offset, carry):
        pl.semaphore_signal(barrier, inc=1, device_id=peer(offset)[1], device_id_type=MESH)
        return carry

    lax.fori_loop(1, PLANE, greet, 0)
    for device in (up, down):
        pl.semaphore_signal(barrier, inc=1, device_id=device, device_id_type=MESH)

    w_copy = pltpu.make_async_copy(w_hbm, w_vmem, w_sem)
    w_copy.start()
    prior_copy = pltpu.make_async_copy(prior_hbm, prior_ref, prior_sem)
    prior_copy.start()

    src_copy.wait()
    for q in range(SLABS):
        cells = src_ref[:, :, q * 128 : (q + 1) * 128].astype(F32)
        slabs[x * SLABS + q] = (cells[0] + cells[1] + cells[2] + cells[3]).astype(BF16)
    slabs[ALL_SLABS] = jnp.zeros((MEM, 128), BF16)

    pl.semaphore_wait(barrier, PLANE + 1)

    own_slabs = slabs.at[pl.ds(x * SLABS, SLABS)]
    for dx in (1, 3, 2):
        pltpu.make_async_remote_copy(
            src_ref=own_slabs, dst_ref=own_slabs, send_sem=ag_send, recv_sem=ag_recv,
            device_id=(band, (x + dx) % NX), device_id_type=MESH,
        ).start()

    wide = (BLOCKS, 128)
    row = lax.broadcasted_iota(I32, wide, 0)
    wanted = (row % NZ) * PLANE + row // NZ
    lane_id = lax.broadcasted_iota(I32, (1, 128), 1)
    low = jnp.full(wide, 1 << 30, I32)
    high = jnp.full(wide, -1, I32)
    for half in range(BLOCKS // 128):
        at = slice(half, half + 1)
        key = (lane_id + 128 * half) * 8192 + slab_ref[at, :] * 32 + tile_ref[at, :]
        named = wanted == dest_ref[at, :]
        low = jnp.minimum(low, jnp.where(named, key, 1 << 30))
        high = jnp.maximum(high, jnp.where(named, key, -1))
    low = jnp.broadcast_to(jnp.min(low, axis=1, keepdims=True), wide)
    high = jnp.broadcast_to(jnp.max(high, axis=1, keepdims=True), wide)
    has_first, has_last = high >= 0, high > low
    first = jnp.where(has_first, low, EMPTY)
    last = jnp.where(has_last, high, EMPTY)
    for half in range(BLOCKS // 128):
        at = slice(half * 128, half * 128 + 128)
        table_vmem[half : half + 1, :] = first[at].T[0:1, :]
        table_vmem[2 + half : 3 + half, :] = last[at].T[0:1, :]
    table_copy = pltpu.make_async_copy(table_vmem, table, table_sem)
    table_copy.start()
    base = (row % NZ) * TILES
    tags = [
        jnp.where(has_first, base + (first & 31), -1).astype(F32).reshape(PLANE, NZ, 128),
        jnp.where(has_last, base + (last & 31), -1).astype(F32).reshape(PLANE, NZ, 128),
    ]
    label_ref[...] = jnp.concatenate(tags, axis=1).astype(BF16)
    labels[me] = label_ref[me]

    def send_labels(offset, carry):
        q2, device = peer(offset)
        pltpu.make_async_remote_copy(
            src_ref=label_ref.at[q2], dst_ref=labels.at[me], send_sem=lab_send, recv_sem=lab_recv,
            device_id=device, device_id_type=MESH,
        ).start()
        return carry

    shape = shape_ref[...]
    lgamma_ref[...] = log_gamma(shape)
    coeff = 1.0 / shape
    series[0] = coeff
    for n in range(1, 65):
        coeff = coeff * (shape + 1.0) / (shape + n)
        series[n] = coeff
    prior_copy.wait()
    for mi in range(MEM // 8):
        for j in range(TILES):
            row = (mi * TILES + j) * 8
            prior_rows[row : row + 8, :] = prior_ref[mi * 8 : mi * 8 + 8, j * 128 : (j + 1) * 128]

    lax.fori_loop(1, PLANE, send_labels, 0)
    table_copy.wait()
    w_copy.wait()
    drain(slabs.at[pl.ds(0, (NX - 1) * SLABS)], ag_recv)

    def pieces(q2):
        for k in range(SLOTS):
            key = table[2 * (k // NZ) + q2 // (128 // NZ), (q2 % (128 // NZ)) * NZ + k % NZ]
            slab = (key >> 5) & 255
            block = key >> 13
            piece = jnp.dot(slabs[slab], w_vmem[block], preferred_element_type=F32)
            stage[pl.ds(k, MEM, stride=SLOTS), :] = piece

    def p1_copy(chunk, offset):
        q2, device = peer(offset)
        return pltpu.make_async_remote_copy(
            src_ref=sendb.at[chunk, q2], dst_ref=recvb.at[chunk, me], send_sem=p1_send.at[chunk],
            recv_sem=p1_recv.at[chunk], device_id=device, device_id_type=MESH,
        )

    rows = MC * SLOTS

    def produce(offset, carry):
        q2, _ = peer(offset)
        pieces(q2)
        for chunk in range(CHUNKS):
            sendb[chunk, q2] = stage[chunk * rows : (chunk + 1) * rows, :].astype(BF16)

        @pl.when(offset > 1)
        def _():
            p1_copy(0, offset - 1).start()

        return carry

    lax.fori_loop(1, PLANE, produce, 0)
    pieces(me)
    for chunk in range(CHUNKS):
        recvb[chunk, me] = stage[chunk * rows : (chunk + 1) * rows, :].astype(BF16)
    p1_copy(0, PLANE - 1).start()

    def send_chunk(step, carry):
        p1_copy(1 + step // (PLANE - 1), 1 + step % (PLANE - 1)).start()
        return carry

    lax.fori_loop(0, (CHUNKS - 1) * (PLANE - 1), send_chunk, 0)

    drain(labels.at[pl.ds(0, PLANE - 1)], lab_recv)
    got = labels[...].astype(F32).reshape(PLANE * SLOTS, 128)
    lane = lax.broadcasted_iota(I32, (PLANE * SLOTS, 128), 1).astype(F32)
    for half in range(NZ * TILES // 128):
        hit = jnp.where(got == lane + 128.0 * half, 1.0, 0.0)
        onehot[half * 128 : (half + 1) * 128, :] = hit.T.astype(BF16)

    def rs_copy(chunk, step, way):
        span = slice(16 * way, 16 * way + 16) if step == 0 else slice(0, TILES)
        return pltpu.make_async_remote_copy(
            src_ref=rs_send.at[way, chunk, step, :, span], dst_ref=rs_recv.at[way, chunk, step, :, span],
            send_sem=rs_send_sem.at[way, chunk, step], recv_sem=rs_recv_sem.at[way, chunk, step],
            device_id=down if way else up, device_id_type=MESH,
        )

    group = 16

    def tail(chunk, g):
        lo = pl.multiple_of(group * g, group)
        cells = pl.ds(lo, group)
        a = shape_ref[cells, :]
        inv_scale = 1.0 / scale_ref[cells, :]
        inv_border = 1.0 / (a + 1.0)

        def member_rows(m):
            member = chunk * MC + m
            return pl.ds((member // 8) * (TILES * 8) + g * (8 * group) + member % 8, group, stride=8)

        remapped = part[chunk, :, pl.ds(pl.multiple_of(z * TILES + group * g, group), group), :]
        remapped = remapped + rs_recv[0, chunk, HALF - 1, :, cells, :].astype(F32)
        remapped = remapped + rs_recv[1, chunk, HALF - 1, :, cells, :].astype(F32)
        season = remapped + jnp.stack([prior_rows[member_rows(m), :] for m in range(MC)])
        for m in range(MC):
            season_rows[member_rows(m), :] = season[m]
        value = season * inv_scale
        border = a + 1.0
        below = value < border
        prefactor = jnp.exp(a * jnp.log(value) - value - lgamma_ref[cells, :])

        ratio = jnp.minimum(value, border) * inv_border
        total = jnp.zeros_like(ratio) + series[64, cells, :]
        for n in range(63, -1, -1):
            total = total * ratio + series[n, cells, :]

        shifted = jnp.clip(value, border, FRACTION_TOP) - a
        quot = 1.0 / (shifted + 129.0)
        for top in range(64, 0, -8):
            older, newer = None, None
            for i in range(top, top - 8, -1):
                step_a = (a - float(i)) * float(i)
                denom = shifted + float(2 * i - 1)
                if newer is None:
                    older, newer = 1.0, denom + step_a * quot
                else:
                    older, newer = newer, denom * newer + step_a * older
            quot = older / newer

        prob = jnp.where(below, total * prefactor, 1.0 - quot * prefactor)
        prob = jnp.clip(prob, PROB_FLOOR, 1.0 - PROB_FLOOR)
        centred = prob - 0.5
        square = centred * centred
        low, high = prob < 0.02425, prob > 0.97575
        root = jnp.sqrt(-2.0 * jnp.log(jnp.where(high, 1.0 - prob, prob)))
        tail_numer = horner(TAIL_NUMER, root)
        numer = jnp.where(low, tail_numer, centred * horner(CENTRAL_NUMER, square))
        numer = jnp.where(high, -tail_numer, numer)
        denom = jnp.where(low | high, horner(TAIL_DENOM, root), horner(CENTRAL_DENOM, square))
        spi = numer / denom
        for m in range(MC):
            spi_rows[member_rows(m), :] = spi[m]

    def gather_sums(chunk):
        drain(recvb.at[chunk, pl.ds(0, PLANE - 1)], p1_recv.at[chunk])
        for m in range(0, MC, 2):
            both = [
                recvb[chunk, :, (m + e) * SLOTS : (m + e + 1) * SLOTS, :].reshape(PLANE * SLOTS, 128)
                for e in range(2)
            ]
            sums = jnp.dot(onehot[...], jnp.concatenate(both, axis=1), preferred_element_type=F32)
            part[chunk, m] = sums[:, :128]
            part[chunk, m + 1] = sums[:, 128:]

    def ring_step(chunk, step):
        hops = HALF - step
        for way in range(2):
            dest = (z + hops) % NZ if way == 0 else (z + NZ - hops) % NZ
            if step == 0:
                at = pl.multiple_of(dest * TILES + 16 * way, 16)
                mine = part[chunk, :, pl.ds(at, 16), :]
                rs_send[way, chunk, 0, :, 16 * way : 16 * way + 16, :] = mine.astype(BF16)
                continue
            rs_copy(chunk, step - 1, way).wait_recv()
            mine = part[chunk, :, pl.ds(pl.multiple_of(dest * TILES, TILES), TILES), :]
            if step == 1:
                other = rs_recv[way, chunk, 0, :, 16 * way : 16 * way + 16, :].astype(F32)
                own_half = mine[:, 16 * way : 16 * way + 16, :] + other
                halves = [own_half, mine[:, 16:, :]] if way == 0 else [mine[:, :16, :], own_half]
                total = jnp.concatenate(halves, axis=1)
            else:
                total = mine + rs_recv[way, chunk, step - 1].astype(F32)
            rs_send[way, chunk, step] = total.astype(BF16)
        for way in range(2):
            rs_copy(chunk, step, way).start()

    def out_copies(mi):
        at = pl.ds(pl.multiple_of(mi * 8, 8), 8)
        return [
            pltpu.make_async_copy(season_ref.at[at], season_hbm.at[at], out_sem.at[0, mi]),
            pltpu.make_async_copy(spi_ref.at[at], spi_hbm.at[at], out_sem.at[1, mi]),
        ]

    def finish(chunk):
        for way in range(2):
            rs_copy(chunk, HALF - 1, way).wait_recv()

        def tail_group(g, inner):
            tail(chunk, g)
            return inner

        lax.fori_loop(0, TILES // group, tail_group, 0)

        @pl.when((chunk + 1) * MC % 8 == 0)
        def _():
            mi = chunk * MC // 8
            at = pl.ds(pl.multiple_of(mi * 8, 8), 8)
            for j in range(TILES):
                rows = pl.ds(pl.multiple_of((mi * TILES + j) * 8, 8), 8)
                season_ref[at, j * 128 : (j + 1) * 128] = season_rows[rows, :]
                spi_ref[at, j * 128 : (j + 1) * 128] = spi_rows[rows, :]
            for copy in out_copies(mi):
                copy.start()

    def iterate(it, carry):
        @pl.when(it < CHUNKS)
        def _():
            gather_sums(it)
            ring_step(it, 0)

        for step in range(HALF - 1, 0, -1):

            @pl.when((it >= step) & (it < CHUNKS + step))
            def _(step=step):
                ring_step(it - step, step)

        @pl.when(it >= HALF)
        def _():
            finish(it - HALF)

        return carry

    lax.fori_loop(0, CHUNKS + HALF, iterate, 0)

    drain(slabs.at[pl.ds(0, (NX - 1) * SLABS)], ag_send)
    drain(labels.at[pl.ds(0, PLANE - 1)], lab_send)

    def settle(chunk, carry):
        drain(sendb.at[chunk, pl.ds(0, PLANE - 1)], p1_send.at[chunk])
        for step in range(HALF):
            for way in range(2):
                rs_copy(chunk, step, way).wait_send()
        return carry

    lax.fori_loop(0, CHUNKS, settle, 0)
    for mi in range(MEM // 8):
        for copy in out_copies(mi):
            copy.wait()


def shards(src_field, weights, block_slab, block_dest, block_tile, prior_total, gamma_shape, gamma_scale):
    vmem = pl.BlockSpec(memory_space=pltpu.VMEM)
    hbm = pl.BlockSpec(memory_space=pl.ANY)
    dma = pltpu.SemaphoreType.DMA
    cells = (TILES, 128)
    return pl.pallas_call(
        kernel,
        out_shape=[jax.ShapeDtypeStruct(prior_total.shape, F32)] * 2,
        in_specs=[vmem, vmem, vmem, hbm, hbm, hbm, vmem, vmem],
        out_specs=[hbm, hbm],
        scratch_shapes=[
            pltpu.VMEM((DAYS, MEM, SLABS * 128), BF16),
            pltpu.VMEM((MEM, TILES * 128), F32),
            pltpu.VMEM((MEM, TILES * 128), F32),
            pltpu.VMEM((MEM, TILES * 128), F32),
            pltpu.VMEM((4, 128), I32),
            pltpu.SMEM((4, 128), I32),
            pltpu.VMEM((PLANE, SLOTS, 128), BF16),
            pltpu.VMEM((TILES, 128), F32),
            pltpu.VMEM((ALL_SLABS + 1, MEM, 128), BF16),
            pltpu.VMEM((BLOCKS, 128, 128), BF16),
            pltpu.VMEM((MEM * SLOTS, 128), F32),
            pltpu.VMEM((CHUNKS, PLANE, MC * SLOTS, 128), BF16),
            pltpu.VMEM((CHUNKS, PLANE, MC * SLOTS, 128), BF16),
            pltpu.VMEM((PLANE, SLOTS, 128), BF16),
            pltpu.VMEM((NZ * TILES, PLANE * SLOTS), BF16),
            pltpu.VMEM((CHUNKS, MC, NZ * TILES, 128), F32),
            pltpu.VMEM((2, CHUNKS, HALF, MC, TILES, 128), BF16),
            pltpu.VMEM((2, CHUNKS, HALF, MC, TILES, 128), BF16),
            pltpu.VMEM((65, TILES, 128), F32),
            pltpu.VMEM((MEM * TILES, 128), F32),
            pltpu.VMEM((MEM * TILES, 128), F32),
            pltpu.VMEM((MEM * TILES, 128), F32),
            dma, dma, dma, dma, dma((2, MEM // 8)), dma, dma, dma, dma, dma((CHUNKS,)), dma((CHUNKS,)), dma((2, CHUNKS, HALF)), dma((2, CHUNKS, HALF)),
        ],
        compiler_params=pltpu.CompilerParams(
            collective_id=0, has_side_effects=True, vmem_limit_bytes=56 * 1024 * 1024
        ),
        name="remap_spi",
    )(
        block_slab.reshape(BLOCKS // 128, 128),
        block_dest.reshape(BLOCKS // 128, 128),
        block_tile.reshape(BLOCKS // 128, 128),
        src_field,
        weights,
        prior_total,
        gamma_shape.reshape(cells),
        gamma_scale.reshape(cells),
    )


def solution(mesh):
    placed = (
        P(None, None, ("band", "tile")),
        P(("band", "tile"), None, None),
        P(("band", "tile")),
        P(("band", "tile"), None),
        P(("band", "tile")),
        P(None, ("band", "tile")),
        P(("band", "tile")),
        P(("band", "tile")),
    )
    return jax.shard_map(
        lambda *arrays: tuple(shards(*arrays)),
        mesh=mesh,
        in_specs=placed,
        out_specs=(P(None, ("band", "tile")), P(None, ("band", "tile"))),
        check_vma=False,
    )
```

```python
import functools

import jax
import jax.numpy as jnp
from jax import lax
from jax.experimental import pallas as pl
from jax.experimental.pallas import tpu as pltpu
from jax.sharding import PartitionSpec as P

MESH = pl.DeviceIdType.MESH
F32, BF16, I32 = jnp.float32, jnp.bfloat16, jnp.int32

PROB_FLOOR = 0.001
CENTRAL_NUMER = (
    -39.69683028665376,
    220.9460984245205,
    -275.9285104469687,
    138.357751867269,
    -30.66479806614716,
    2.506628277459239,
)
CENTRAL_DENOM = (
    -54.47609879822406,
    161.5858368580409,
    -155.6989798598866,
    66.80131188771972,
    -13.28068155288572,
    1.0,
)
TAIL_NUMER = (
    -0.007784894002430293,
    -0.3223964580411365,
    -2.400758277161838,
    -2.549671010429402,
    4.374664141464968,
    2.938163982698783,
)
TAIL_DENOM = (0.007784695709041462, 0.3224671290700398, 2.445134137142996, 3.754408661907416, 1.0)

NZ, NY, NC, NX = 8, 4, 2, 4
PLANE = NY * NC * NX
DAYS, MEM, TILES, SLABS, BLOCKS = 4, 32, 32, 32, 256
SLOTS = 2 * NZ
ALL_SLABS = NX * SLABS
CHUNKS = 8
MC = MEM // CHUNKS
HALF = NZ // 2
FIRST = 2
FRACTION_TOP = 512.0
EMPTY = ALL_SLABS << 5
LANCZOS_BASE = 0.99999999999980993227684700473478
LANCZOS = (
    676.520368121885098567009190444019,
    -1259.13921672240287047156078755283,
    771.3234287776530788486528258894,
    -176.61502916214059906584551354,
    12.507343278686904814458936853,
    -0.13857109526572011689554707,
    9.984369578019570859563e-6,
    1.50563273514931155834e-7,
)


def horner(coeffs, value):
    total = coeffs[0]
    for coeff in coeffs[1:]:
        total = total * value + coeff
    return total


def log_gamma(shape):
    less = shape - 1.0
    total = LANCZOS_BASE
    for i, coeff in enumerate(LANCZOS):
        total = total + coeff / (less + float(i + 1))
    shifted = less + 7.5
    return 0.9189385332046727 + (less + 0.5) * jnp.log(shifted) - shifted + jnp.log(total)


def drain(ref, sem):
    pltpu.make_async_copy(ref, ref, sem).wait()


def kernel(
    slab_hbm, dest_hbm, tile_hbm, src_hbm, w_hbm, prior_hbm, shape_hbm, scale_hbm,
    season_hbm, spi_hbm,
    slab_ref, dest_ref, tile_ref, shape_ref, scale_ref, src_ref, prior_ref, season_ref, spi_ref, table_vmem, table, label_ref, lgamma_ref,
    slabs, w_vmem, stage, sendb, recvb, labels, onehot, part, rs_send, rs_recv, series, prior_rows, season_rows, spi_rows,
    small_sem, w_sem, src_sem, prior_sem, table_sem, out_sem, ag_send, ag_recv, lab_send, lab_recv, p1_send, p1_recv, rs_send_sem, rs_recv_sem,
):
    band = lax.axis_index("band")
    x = lax.axis_index("tile")
    core = band % NC
    y = (band // NC) % NY
    z = band // (NC * NY)
    me = (y * NC + core) * NX + x

    def peer(offset):
        y2 = lax.rem(y + offset + lax.div(offset, NX), NY)
        c2 = lax.rem(core + lax.div(offset, NX * NY), NC)
        x2 = lax.rem(x + offset, NX)
        return (y2 * NC + c2) * NX + x2, ((z * NY + y2) * NC + c2, x2)

    def z_device(z2):
        return ((z2 * NY + y) * NC + core, x)

    up, down = z_device((z + 1) % NZ), z_device((z + NZ - 1) % NZ)

    src_copy = pltpu.make_async_copy(src_hbm, src_ref, src_sem)
    src_copy.start()
    barrier = pltpu.get_barrier_semaphore()

    def greet(offset, carry):
        pl.semaphore_signal(barrier, inc=1, device_id=peer(offset)[1], device_id_type=MESH)
        return carry

    lax.fori_loop(1, PLANE, greet, 0)
    for device in (up, down):
        pl.semaphore_signal(barrier, inc=1, device_id=device, device_id_type=MESH)

    w_copy = pltpu.make_async_copy(w_hbm, w_vmem, w_sem)
    w_copy.start()
    prior_copy = pltpu.make_async_copy(prior_hbm, prior_ref, prior_sem)
    prior_copy.start()
    small_copies = [
        pltpu.make_async_copy(there, here, small_sem.at[i])
        for i, (there, here) in enumerate(
            [(slab_hbm, slab_ref), (dest_hbm, dest_ref), (tile_hbm, tile_ref), (shape_hbm, shape_ref), (scale_hbm, scale_ref)]
        )
    ]
    for copy in small_copies:
        copy.start()

    src_copy.wait()
    for q in range(SLABS):
        cells = src_ref[:, :, q * 128 : (q + 1) * 128].astype(F32)
        slabs[x * SLABS + q] = (cells[0] + cells[1] + cells[2] + cells[3]).astype(BF16)
    slabs[ALL_SLABS] = jnp.zeros((MEM, 128), BF16)

    pl.semaphore_wait(barrier, PLANE + 1)

    half_slabs = SLABS // 2

    def ag_copy(owner, half, way, sem):
        at = slabs.at[pl.ds(owner * SLABS + half * half_slabs, half_slabs)]
        x2 = (x + NX - 1) % NX if way else (x + 1) % NX
        return pltpu.make_async_remote_copy(
            src_ref=at, dst_ref=at, send_sem=ag_send.at[sem], recv_sem=ag_recv.at[sem],
            device_id=(band, x2), device_id_type=MESH,
        )

    own_copies = [ag_copy(x, way if turn == 0 else 1 - way, way, 2 * way + turn) for turn in range(2) for way in range(2)]
    for copy in own_copies:
        copy.start()

    for copy in small_copies:
        copy.wait()
    wide = (BLOCKS, 128)
    row = lax.broadcasted_iota(I32, wide, 0)
    wanted = (row % NZ) * PLANE + row // NZ
    lane_id = lax.broadcasted_iota(I32, (1, 128), 1)
    low = jnp.full(wide, 1 << 30, I32)
    high = jnp.full(wide, -1, I32)
    for half in range(BLOCKS // 128):
        at = slice(half, half + 1)
        key = (lane_id + 128 * half) * 8192 + slab_ref[at, :] * 32 + tile_ref[at, :]
        named = wanted == dest_ref[at, :]
        low = jnp.minimum(low, jnp.where(named, key, 1 << 30))
        high = jnp.maximum(high, jnp.where(named, key, -1))
    low = jnp.broadcast_to(jnp.min(low, axis=1, keepdims=True), wide)
    high = jnp.broadcast_to(jnp.max(high, axis=1, keepdims=True), wide)
    has_first, has_last = high >= 0, high > low
    first = jnp.where(has_first, low, EMPTY)
    last = jnp.where(has_last, high, EMPTY)
    for half in range(BLOCKS // 128):
        at = slice(half * 128, half * 128 + 128)
        table_vmem[half : half + 1, :] = first[at].T[0:1, :]
        table_vmem[2 + half : 3 + half, :] = last[at].T[0:1, :]
    table_copy = pltpu.make_async_copy(table_vmem, table, table_sem)
    table_copy.start()
    base = (row % NZ) * TILES
    tags = [
        jnp.where(has_first, base + (first & 31), -1).astype(F32).reshape(PLANE, NZ, 128),
        jnp.where(has_last, base + (last & 31), -1).astype(F32).reshape(PLANE, NZ, 128),
    ]
    label_ref[...] = jnp.concatenate(tags, axis=1).astype(BF16)
    labels[me] = label_ref[me]

    def send_labels(offset, carry):
        q2, device = peer(offset)
        pltpu.make_async_remote_copy(
            src_ref=label_ref.at[q2], dst_ref=labels.at[me], send_sem=lab_send, recv_sem=lab_recv,
            device_id=device, device_id_type=MESH,
        ).start()
        return carry

    shape = shape_ref[...]
    lgamma_ref[...] = log_gamma(shape)
    coeff = 1.0 / shape
    series[0] = coeff
    for n in range(1, 65):
        coeff = coeff * (shape + 1.0) / (shape + n)
        series[n] = coeff
    prior_copy.wait()
    for mi in range(MEM // 8):
        for j in range(TILES):
            row = (mi * TILES + j) * 8
            prior_rows[row : row + 8, :] = prior_ref[mi * 8 : mi * 8 + 8, j * 128 : (j + 1) * 128]

    passed_on = []
    for way in range(2):
        own_copies[way].wait_recv()
        owner = (x + 1) % NX if way else (x + NX - 1) % NX
        passed_on.append(ag_copy(owner, way, way, 4 + way))
        passed_on[way].start()
    lax.fori_loop(1, PLANE, send_labels, 0)
    table_copy.wait()
    w_copy.wait()
    for copy in own_copies[2:] + passed_on:
        copy.wait_recv()

    def pieces(q2):
        for k in range(SLOTS):
            key = table[2 * (k // NZ) + q2 // (128 // NZ), (q2 % (128 // NZ)) * NZ + k % NZ]
            slab = (key >> 5) & 255
            block = key >> 13
            piece = jnp.dot(slabs[slab], w_vmem[block], preferred_element_type=F32)
            stage[pl.ds(k, MEM, stride=SLOTS), :] = piece

    def p1_copy(chunk, offset):
        q2, device = peer(offset)
        return pltpu.make_async_remote_copy(
            src_ref=sendb.at[chunk, q2], dst_ref=recvb.at[chunk, me], send_sem=p1_send.at[chunk],
            recv_sem=p1_recv.at[chunk], device_id=device, device_id_type=MESH,
        )

    rows = MC * SLOTS

    def produce(offset, carry):
        q2, _ = peer(offset)
        pieces(q2)
        for chunk in range(CHUNKS):
            sendb[chunk, q2] = stage[chunk * rows : (chunk + 1) * rows, :].astype(BF16)

        @pl.when(offset > 1)
        def _():
            for chunk in range(FIRST):
                p1_copy(chunk, offset - 1).start()

        return carry

    lax.fori_loop(1, PLANE, produce, 0)
    pieces(me)
    for chunk in range(CHUNKS):
        recvb[chunk, me] = stage[chunk * rows : (chunk + 1) * rows, :].astype(BF16)
    for chunk in range(FIRST):
        p1_copy(chunk, PLANE - 1).start()

    def send_chunk(chunk):
        def send(offset, carry):
            p1_copy(chunk, offset).start()
            return carry

        lax.fori_loop(1, PLANE, send, 0)

    send_chunk(FIRST)

    drain(labels.at[pl.ds(0, PLANE - 1)], lab_recv)
    got = labels[...].astype(F32).reshape(PLANE * SLOTS, 128)
    lane = lax.broadcasted_iota(I32, (PLANE * SLOTS, 128), 1).astype(F32)
    for half in range(NZ * TILES // 128):
        hit = jnp.where(got == lane + 128.0 * half, 1.0, 0.0)
        onehot[half * 128 : (half + 1) * 128, :] = hit.T.astype(BF16)

    def rs_copy(chunk, step, way):
        span = slice(16 * way, 16 * way + 16) if step == 0 else slice(0, TILES)
        return pltpu.make_async_remote_copy(
            src_ref=rs_send.at[way, chunk, step, :, span], dst_ref=rs_recv.at[way, chunk, step, :, span],
            send_sem=rs_send_sem.at[way, chunk, step], recv_sem=rs_recv_sem.at[way, chunk, step],
            device_id=down if way else up, device_id_type=MESH,
        )

    group = 16

    def tail(chunk, g):
        lo = pl.multiple_of(group * g, group)
        cells = pl.ds(lo, group)
        a = shape_ref[cells, :]
        inv_scale = 1.0 / scale_ref[cells, :]
        inv_border = 1.0 / (a + 1.0)

        def member_rows(m):
            member = chunk * MC + m
            return pl.ds((member // 8) * (TILES * 8) + g * (8 * group) + member % 8, group, stride=8)

        remapped = part[chunk, :, pl.ds(pl.multiple_of(z * TILES + group * g, group), group), :]
        remapped = remapped + rs_recv[0, chunk, HALF - 1, :, cells, :].astype(F32)
        remapped = remapped + rs_recv[1, chunk, HALF - 1, :, cells, :].astype(F32)
        season = remapped + jnp.stack([prior_rows[member_rows(m), :] for m in range(MC)])
        for m in range(MC):
            season_rows[member_rows(m), :] = season[m]
        value = season * inv_scale
        border = a + 1.0
        below = value < border
        prefactor = jnp.exp(a * jnp.log(value) - value - lgamma_ref[cells, :])

        ratio = jnp.minimum(value, border) * inv_border
        total = jnp.zeros_like(ratio) + series[64, cells, :]
        for n in range(63, -1, -1):
            total = total * ratio + series[n, cells, :]

        shifted = jnp.clip(value, border, FRACTION_TOP) - a
        quot = 1.0 / (shifted + 129.0)
        for top in range(64, 0, -8):
            older, newer = None, None
            for i in range(top, top - 8, -1):
                step_a = (a - float(i)) * float(i)
                denom = shifted + float(2 * i - 1)
                if newer is None:
                    older, newer = 1.0, denom + step_a * quot
                else:
                    older, newer = newer, denom * newer + step_a * older
            quot = older / newer

        prob = jnp.where(below, total * prefactor, 1.0 - quot * prefactor)
        prob = jnp.clip(prob, PROB_FLOOR, 1.0 - PROB_FLOOR)
        centred = prob - 0.5
        square = centred * centred
        low, high = prob < 0.02425, prob > 0.97575
        root = jnp.sqrt(-2.0 * jnp.log(jnp.where(high, 1.0 - prob, prob)))
        tail_numer = horner(TAIL_NUMER, root)
        numer = jnp.where(low, tail_numer, centred * horner(CENTRAL_NUMER, square))
        numer = jnp.where(high, -tail_numer, numer)
        denom = jnp.where(low | high, horner(TAIL_DENOM, root), horner(CENTRAL_DENOM, square))
        spi = numer / denom
        for m in range(MC):
            spi_rows[member_rows(m), :] = spi[m]

    def gather_sums(chunk):
        drain(recvb.at[chunk, pl.ds(0, PLANE - 1)], p1_recv.at[chunk])
        for m in range(0, MC, 2):
            both = [
                recvb[chunk, :, (m + e) * SLOTS : (m + e + 1) * SLOTS, :].reshape(PLANE * SLOTS, 128)
                for e in range(2)
            ]
            sums = jnp.dot(onehot[...], jnp.concatenate(both, axis=1), preferred_element_type=F32)
            part[chunk, m] = sums[:, :128]
            part[chunk, m + 1] = sums[:, 128:]

    def ring_step(chunk, step):
        hops = HALF - step
        for way in range(2):
            dest = (z + hops) % NZ if way == 0 else (z + NZ - hops) % NZ
            if step == 0:
                at = pl.multiple_of(dest * TILES + 16 * way, 16)
                mine = part[chunk, :, pl.ds(at, 16), :]
                rs_send[way, chunk, 0, :, 16 * way : 16 * way + 16, :] = mine.astype(BF16)
                continue
            rs_copy(chunk, step - 1, way).wait_recv()
            mine = part[chunk, :, pl.ds(pl.multiple_of(dest * TILES, TILES), TILES), :]
            if step == 1:
                other = rs_recv[way, chunk, 0, :, 16 * way : 16 * way + 16, :].astype(F32)
                own_half = mine[:, 16 * way : 16 * way + 16, :] + other
                halves = [own_half, mine[:, 16:, :]] if way == 0 else [mine[:, :16, :], own_half]
                total = jnp.concatenate(halves, axis=1)
            else:
                total = mine + rs_recv[way, chunk, step - 1].astype(F32)
            rs_send[way, chunk, step] = total.astype(BF16)
        for way in range(2):
            rs_copy(chunk, step, way).start()

    def out_copies(mi):
        at = pl.ds(pl.multiple_of(mi * 8, 8), 8)
        return [
            pltpu.make_async_copy(season_ref.at[at], season_hbm.at[at], out_sem.at[0, mi]),
            pltpu.make_async_copy(spi_ref.at[at], spi_hbm.at[at], out_sem.at[1, mi]),
        ]

    def finish(chunk):
        for way in range(2):
            rs_copy(chunk, HALF - 1, way).wait_recv()

        def tail_group(g, inner):
            tail(chunk, g)
            return inner

        lax.fori_loop(0, TILES // group, tail_group, 0)

        @pl.when((chunk + 1) * MC % 8 == 0)
        def _():
            mi = chunk * MC // 8
            at = pl.ds(pl.multiple_of(mi * 8, 8), 8)
            for j in range(TILES):
                rows = pl.ds(pl.multiple_of((mi * TILES + j) * 8, 8), 8)
                season_ref[at, j * 128 : (j + 1) * 128] = season_rows[rows, :]
                spi_ref[at, j * 128 : (j + 1) * 128] = spi_rows[rows, :]
            for copy in out_copies(mi):
                copy.start()

    def iterate(it, carry):
        @pl.when(it < CHUNKS - FIRST - 1)
        def _():
            send_chunk(it + FIRST + 1)

        @pl.when(it < CHUNKS)
        def _():
            gather_sums(it)
            ring_step(it, 0)

        for step in range(1, HALF):

            @pl.when((it >= step) & (it < CHUNKS + step))
            def _(step=step):
                ring_step(it - step, step)

        @pl.when(it >= HALF)
        def _():
            finish(it - HALF)

        return carry

    lax.fori_loop(0, CHUNKS + HALF, iterate, 0)

    for copy in own_copies + passed_on:
        copy.wait_send()
    drain(labels.at[pl.ds(0, PLANE - 1)], lab_send)

    def settle(chunk, carry):
        drain(sendb.at[chunk, pl.ds(0, PLANE - 1)], p1_send.at[chunk])
        for step in range(HALF):
            for way in range(2):
                rs_copy(chunk, step, way).wait_send()
        return carry

    lax.fori_loop(0, CHUNKS, settle, 0)
    for mi in range(MEM // 8):
        for copy in out_copies(mi):
            copy.wait()


def shards(src_field, weights, block_slab, block_dest, block_tile, prior_total, gamma_shape, gamma_scale):
    dma = pltpu.SemaphoreType.DMA
    cells = (TILES, 128)
    return pl.pallas_call(
        kernel,
        out_shape=[jax.ShapeDtypeStruct(prior_total.shape, F32)] * 2,
        in_specs=[pl.BlockSpec(memory_space=pl.ANY)] * 8,
        out_specs=[pl.BlockSpec(memory_space=pl.ANY)] * 2,
        scratch_shapes=[
            pltpu.VMEM((BLOCKS // 128, 128), I32),
            pltpu.VMEM((BLOCKS // 128, 128), I32),
            pltpu.VMEM((BLOCKS // 128, 128), I32),
            pltpu.VMEM(cells, F32),
            pltpu.VMEM(cells, F32),
            pltpu.VMEM((DAYS, MEM, SLABS * 128), BF16),
            pltpu.VMEM((MEM, TILES * 128), F32),
            pltpu.VMEM((MEM, TILES * 128), F32),
            pltpu.VMEM((MEM, TILES * 128), F32),
            pltpu.VMEM((4, 128), I32),
            pltpu.SMEM((4, 128), I32),
            pltpu.VMEM((PLANE, SLOTS, 128), BF16),
            pltpu.VMEM((TILES, 128), F32),
            pltpu.VMEM((ALL_SLABS + 1, MEM, 128), BF16),
            pltpu.VMEM((BLOCKS, 128, 128), BF16),
            pltpu.VMEM((MEM * SLOTS, 128), F32),
            pltpu.VMEM((CHUNKS, PLANE, MC * SLOTS, 128), BF16),
            pltpu.VMEM((CHUNKS, PLANE, MC * SLOTS, 128), BF16),
            pltpu.VMEM((PLANE, SLOTS, 128), BF16),
            pltpu.VMEM((NZ * TILES, PLANE * SLOTS), BF16),
            pltpu.VMEM((CHUNKS, MC, NZ * TILES, 128), F32),
            pltpu.VMEM((2, CHUNKS, HALF, MC, TILES, 128), BF16),
            pltpu.VMEM((2, CHUNKS, HALF, MC, TILES, 128), BF16),
            pltpu.VMEM((65, TILES, 128), F32),
            pltpu.VMEM((MEM * TILES, 128), F32),
            pltpu.VMEM((MEM * TILES, 128), F32),
            pltpu.VMEM((MEM * TILES, 128), F32),
            dma((5,)), dma, dma, dma, dma, dma((2, MEM // 8)), dma((6,)), dma((6,)), dma, dma, dma((CHUNKS,)), dma((CHUNKS,)), dma((2, CHUNKS, HALF)), dma((2, CHUNKS, HALF)),
        ],
        compiler_params=pltpu.CompilerParams(
            collective_id=0, has_side_effects=True, vmem_limit_bytes=34 * 1024 * 1024
        ),
        name="remap_spi",
    )(*[
        pltpu.with_memory_space_constraint(array, pltpu.HBM)
        for array in (
            block_slab.reshape(BLOCKS // 128, 128),
            block_dest.reshape(BLOCKS // 128, 128),
            block_tile.reshape(BLOCKS // 128, 128),
            src_field,
            weights,
            prior_total,
            gamma_shape.reshape(cells),
            gamma_scale.reshape(cells),
        )
    ])


def solution(mesh):
    placed = (
        P(None, None, ("band", "tile")),
        P(("band", "tile"), None, None),
        P(("band", "tile")),
        P(("band", "tile"), None),
        P(("band", "tile")),
        P(None, ("band", "tile")),
        P(("band", "tile")),
        P(("band", "tile")),
    )
    return jax.shard_map(
        lambda *arrays: tuple(shards(*arrays)),
        mesh=mesh,
        in_specs=placed,
        out_specs=(P(None, ("band", "tile")), P(None, ("band", "tile"))),
        check_vma=False,
    )
```
